128 devices in a mesh: blk: 16 (over x, y_hi, core), grp: 8 (over z, y_lo).
Axes of the slice: x: 4, y: 4 (y_hi: 2, y_lo: 2; y = y_hi * 2 + y_lo), z: 4, core: 2. Of those that a mesh axis runs over, the one named last changes fastest.
Arguments:
- raw_panels: bfloat16 [8, 2048, 8192], P('grp', 'blk'), may hold values from -0.375 to 0.375
- metric: bfloat16 [1024, 1024], replicated, may hold values from -0.1875 to 0.1875
- tile_pairs: int32 [224, 2], P('blk'), may hold values from 0 to 15, as said below
- owners: int32 [224, 1], P('blk'), may hold values from 0 to 15; in each aligned block of 14 rows (0 to 13, 14 to 27, ...) at most 2 rows name the same one
- group_mask: int32 [224, 8], P('blk', 'grp'), may hold values 0 or 1
Outputs:
- owned_tiles: float32 [16, 16, 2, 128, 128], P('blk', None, None, 'grp')
The draws below stay inside these ranges and needn't reach their ends.
Inputs may be any that keep to these rules, and one draw needn't show every extreme that they name: `tile_pairs`: tile rows of source s (rows s * 14 to s * 14 + 13) have first entry s, the basis block held by index s of blk; the second entry differs from the first. `owners`: in each aligned block of 14 rows (one source) no owner appears more than 2 times.
All inputs are finite; a program needn't handle non-finite values. No bound on the sum of `group_mask` on one device may be relied on, other than what follows from the above.
Results may differ from the reference program's by a relative error of at most 0.0029.
Values may be sent and summed in bfloat16 or wider, within the bound.
A program may use at most 128 MiB of HBM per device.

```python
import math
import jax
import jax.numpy as jnp
import numpy as np
from jax import lax

NAUX = 1024
OCC = 8
TILE = 128
TILE_DEV = 14
GROUPS = 8
NBAS = 2048
LOCAL = 1
NBLOCKS = 16
NTILE = 224
CAP = 2
N_BLK = 16


def draw_tile_pairs(key, part):
    key_local = jax.random.fold_in(key, 11)
    key_step = jax.random.fold_in(key, 23)
    device_of = jnp.arange(NTILE) // TILE_DEV
    local = jax.random.randint(key_local, (NTILE,), 0, LOCAL)
    first = device_of * LOCAL + local
    step = jax.random.randint(key_step, (NTILE,), 1, NBLOCKS)
    second = (first + step) % NBLOCKS
    return jnp.stack([first, second], axis=1).astype(jnp.int32)


def plant(array, key, smallest, largest):
    spot = [jax.random.randint(jax.random.fold_in(key, axis), (), 0, length) for axis, length in enumerate(array.shape)]
    longest = array.shape.index(max(array.shape))
    beside = spot[:longest] + [(spot[longest] + 1) % array.shape[longest]] + spot[longest + 1:]
    return array.at[tuple(spot)].set(smallest).at[tuple(beside)].set(largest)


def shard_levels(own_key, extent, cuts, low, top_value):
    gain, own = 1.0, jax.random.fold_in(own_key, 6)
    for axis_at, shards_of in cuts:
        heights = jnp.exp(jax.random.uniform(jax.random.fold_in(own, axis_at), (shards_of,), jnp.float32, low / len(cuts), top_value / len(cuts)))
        gain = gain * jnp.repeat(heights, extent[axis_at] // shards_of).reshape([-1 if axis == axis_at else 1 for axis in range(len(extent))])
    return gain


def assign_block(key, own, number, rows, count, top, most, skew):
    order = jax.random.permutation(key, count)
    crowded, ordinary = portions_of(count, rows * top, most, skew, True), portions_of(count, rows * top, most, skew, False)
    places = jnp.arange(count)

    def named(tallies, rotation):
        used = int((tallies > 0).sum())
        fixed = max(1, used // 4)
        moved = fixed + (places - fixed + rotation * (used - fixed)) % max(1, count - fixed)
        return jnp.zeros((count,), jnp.int32).at[order[jnp.where(places < fixed, places, moved)]].set(jnp.asarray(tallies, jnp.int32))

    tallies = jnp.where(number % 4 == 0, named(crowded, number // 4), named(ordinary, number - number // 4 - 1))
    mixed = jax.random.permutation(jax.random.fold_in(own, 3), count)
    source_of, receiver = mixed[0:count // 2 * 2:2], mixed[1:count // 2 * 2:2]
    room = jnp.minimum(tallies[source_of] - 1, most - tallies[receiver]) // 2
    room = jnp.where((source_of == order[0]) | (receiver == order[0]) | (tallies[receiver] == 0), 0, jnp.maximum(room, 0))
    moved = jax.random.randint(jax.random.fold_in(own, 4), (count // 2,), 0, 1 << 20) % (room + 1)
    tallies = tallies.at[source_of].add(-moved).at[receiver].add(moved)
    items = jnp.searchsorted(jnp.cumsum(tallies), jnp.arange(rows * top), side="right").astype(jnp.int32)
    table = items.reshape(top, rows).T
    table = table[jax.random.permutation(jax.random.fold_in(own, 1), rows)]
    rotation = jax.random.randint(jax.random.fold_in(own, 2), (rows, 1), 0, top)
    return jnp.take_along_axis(table, (jnp.arange(top)[None, :] + rotation) % top, axis=1)


def portions_of(number_of, total, reach, slope, full):
    portions = [(1 << 20) // math.isqrt(grade ** slope) + 1 for grade in range(1, number_of + 1)]
    largest = reach if full else min(reach, max(-(-total // number_of), total * portions[0] // sum(portions)))
    least = 1 if total - largest >= number_of - 1 else 0
    given, spare = [largest] + [least] * (number_of - 1), total - largest - least * (number_of - 1)
    while spare > 0:
        free = [i for i in range(1, number_of) if given[i] < largest] or [i for i in range(1, number_of) if given[i] < reach]
        whole, left = sum([portions[i] for i in free]), spare
        for i in free:
            more = min(reach - given[i], max(1, left * portions[i] // whole), spare)
            given[i] = given[i] + more
            spare = spare - more
    return np.array(given)


def noise(key, extent, width, reach, pieces=(), dtype=jnp.bfloat16):
    values = width * jax.random.normal(key, extent, jnp.float32)
    if pieces:
        values = values * shard_levels(key, extent, pieces, -0.22, 0.18)
    return jnp.clip(values, -reach, reach).astype(dtype)


def setup_inputs(seed: int = 0) -> dict:
    key_list = jax.random.split(jax.random.key(seed), 6)
    raw_panels = noise(key_list[0], (GROUPS, NBAS, OCC * NAUX), ((NAUX * OCC * GROUPS) ** -0.25), 0.375, ((0, 8), (1, 16)))
    metric = noise(key_list[1], (NAUX, NAUX), NAUX ** -0.5, 0.1875)
    tile_pairs = draw_tile_pairs(jax.random.fold_in(key_list[5], 71), 0)
    owners_keys = jax.random.split(jax.random.fold_in(key_list[3], 1), NTILE // TILE_DEV)
    owners_turns = jax.random.permutation(jax.random.fold_in(key_list[3], 3), NTILE // TILE_DEV)
    owners = jax.vmap(lambda own, number: assign_block(jax.random.fold_in(key_list[3], 2), own, number, TILE_DEV, N_BLK, 1, CAP, 2))(owners_keys, owners_turns).reshape((NTILE, 1))
    group_mask = plant((jax.random.randint(key_list[4], (NTILE, GROUPS), 0, 5) < 3).astype(jnp.int32), jax.random.fold_in(key_list[4], 1), 0, 1)
    return {"raw_panels": raw_panels, "metric": metric, "tile_pairs": tile_pairs, "owners": owners, "group_mask": group_mask}


def reference(raw_panels, metric, tile_pairs, owners, group_mask):
    def transform(raw):
        flat = raw.reshape(NBAS * OCC, NAUX)
        fitted = lax.dot_general(flat, metric, (((1,), (1,)), ((), ())), preferred_element_type=jnp.float32)
        return fitted.astype(jnp.bfloat16).reshape(NBAS, OCC * NAUX)

    panels = lax.map(transform, raw_panels)
    weights = group_mask.astype(jnp.float32)

    def one_tile(item):
        pair, weight = item
        rows_mu = lax.dynamic_slice_in_dim(panels, (pair[0] * TILE).astype(jnp.int32), TILE, 1)
        rows_nu = lax.dynamic_slice_in_dim(panels, (pair[1] * TILE).astype(jnp.int32), TILE, 1)
        prods = jnp.einsum("gmk,gnk->gmn", rows_mu.astype(jnp.float32), rows_nu.astype(jnp.float32))
        return jnp.einsum("g,gmn->mn", weight, prods)

    tiles = lax.map(one_tile, (tile_pairs, weights))
    owner_ids = owners[:, 0].reshape(N_BLK, TILE_DEV)
    labels = jnp.arange(N_BLK).astype(jnp.int32)
    hits = (owner_ids[:, :, None] == labels[None, None, :]).astype(jnp.int32)
    before = jnp.cumsum(hits, axis=1) - hits
    slots = jnp.sum(before * hits, axis=2).reshape(-1).astype(jnp.int32)
    sources = (jnp.arange(N_BLK * TILE_DEV) // TILE_DEV).astype(jnp.int32)
    result = jnp.zeros((N_BLK, N_BLK, CAP, TILE, TILE), jnp.float32)
    return result.at[owners[:, 0], sources, slots].set(tiles)
```

```python
import jax
import jax.numpy as jnp
from jax import lax
from jax.experimental import pallas as pl
from jax.experimental.pallas import tpu as pltpu
from jax.sharding import PartitionSpec as P

MESH = pl.DeviceIdType.MESH
F32, BF16 = jnp.float32, jnp.bfloat16

CHIPS = 8
BLKS = 16
GRPS = 8
T = 128
K = 1024
HALF = 8
SLOTS = 2
ROWS = T // GRPS


def dot_t(a, b):
    return lax.dot_general(a, b, (((1,), (1,)), ((), ())), preferred_element_type=F32)


def kernel(
    raw, metric, pairs, owners, mask, out,
    met, rbuf, fbuf, sbuf, pbuf, xs, xall, ybuf, zbuf, acc, obuf, tbl,
    msem, lsem, asend, arecv, fsend, frecv, psend, precv, xsend, xrecv, ysend, yrecv, osend, orecv, osem,
):
    me = lax.axis_index("blk")
    grp = lax.axis_index("grp")
    chip, core = me // 2, me % 2
    cx, cy = chip // 2, chip % 2
    tiles = pairs.shape[1]

    def chip_to(k):
        return ((cx + k // 2) % 4) * 2 + (cy + k % 2) % 2

    def chip_from(k):
        return ((cx + 4 - k // 2) % 4) * 2 + (cy + k % 2) % 2

    fetch_metric = pltpu.make_async_copy(metric, met, msem)
    fetch_metric.start()
    own = pltpu.make_async_copy(raw.at[:, pl.ds(pl.multiple_of(chip * K, K), K)], rbuf.at[0], lsem)
    own.start()

    barrier = pltpu.get_barrier_semaphore()
    for step in range(1, BLKS):
        pl.semaphore_signal(barrier, inc=1, device_id=((me + step) % BLKS, grp), device_id_type=MESH)
    for step in range(1, GRPS):
        pl.semaphore_signal(barrier, inc=1, device_id=(me, (grp + step) % GRPS), device_id_type=MESH)
    pl.semaphore_wait(barrier, BLKS - 1 + GRPS - 1)

    def raw_copy(k):
        target = chip_to(k)
        return pltpu.make_async_remote_copy(
            src_ref=raw.at[:, pl.ds(pl.multiple_of(target * K, K), K)],
            dst_ref=rbuf.at[k],
            send_sem=asend.at[k],
            recv_sem=arecv.at[k],
            device_id=(target * 2 + core, grp),
            device_id_type=MESH,
        )

    for k in range(1, CHIPS):
        raw_copy(k).start()

    def find(o, carry):
        seen, first, second = jnp.int32(0), jnp.int32(tiles), jnp.int32(tiles)
        for t in range(tiles):
            hit = (owners[0, t] == o).astype(jnp.int32)
            first = first + hit * (seen == 0).astype(jnp.int32) * (t - tiles)
            second = second + hit * (seen == 1).astype(jnp.int32) * (t - tiles)
            seen = seen + hit
        tbl[o * 2] = first
        tbl[o * 2 + 1] = second
        return carry

    lax.fori_loop(0, BLKS, find, 0)

    def fitted_copy(k):
        block = fbuf.at[chip_from(k) * 2 + core]
        return pltpu.make_async_remote_copy(
            src_ref=block,
            dst_ref=block,
            send_sem=fsend.at[k],
            recv_sem=frecv.at[k],
            device_id=(chip * 2 + 1 - core, grp),
            device_id_type=MESH,
        )

    def fitted_arrival(k):
        block = fbuf.at[chip_from(k) * 2 + 1 - core]
        return pltpu.make_async_remote_copy(
            src_ref=block,
            dst_ref=block,
            send_sem=fsend.at[k],
            recv_sem=frecv.at[k],
            device_id=(chip * 2 + 1 - core, grp),
            device_id_type=MESH,
        )

    fetch_metric.wait()
    own.wait()

    def fit(k, carry):
        @pl.when(k > 0)
        def _():
            raw_copy(k).wait_recv()

        fbuf[chip_from(k) * 2 + core] = dot_t(rbuf[k], met[...]).astype(BF16)
        fitted_copy(k).start()
        return carry

    lax.fori_loop(0, CHIPS, fit, 0)
    for k in range(CHIPS):
        fitted_arrival(k).wait_recv()

    def partial_copy(k):
        return pltpu.make_async_remote_copy(
            src_ref=sbuf.at[k],
            dst_ref=pbuf.at[k],
            send_sem=psend.at[k],
            recv_sem=precv.at[k],
            device_id=(chip_to(k) * 2 + core, grp),
            device_id_type=MESH,
        )

    def multiply(step, carry):
        k = CHIPS - 1 - step
        reducer = chip_to(k) * 2 + core
        right = fbuf[reducer]
        for j in range(1, HALF + 1):
            sbuf[k, j - 1] = dot_t(fbuf[(reducer + j) % BLKS], right).astype(BF16)

        @pl.when(k > 0)
        def _():
            partial_copy(k).start()

        return carry

    lax.fori_loop(0, CHIPS, multiply, 0)

    def cross_copy(j):
        return pltpu.make_async_remote_copy(
            src_ref=xs.at[j],
            dst_ref=xall.at[j],
            send_sem=xsend.at[j],
            recv_sem=xrecv.at[j],
            device_id=((me + j) % BLKS, grp),
            device_id_type=MESH,
        )

    for k in range(1, CHIPS):
        partial_copy(k).wait_recv()
    for j in range(1, HALF + 1):
        total = sbuf[0, j - 1].astype(F32)
        for k in range(1, CHIPS):
            total = total + pbuf[k, j - 1].astype(F32)
        if j < HALF:
            xs[j] = total.astype(BF16)
            cross_copy(j).start()
        xall[BLKS - j] = total.T.astype(BF16)
    for j in range(1, HALF):
        cross_copy(j).wait_recv()

    def slice_copy(step):
        target = (grp + step) % GRPS
        return pltpu.make_async_remote_copy(
            src_ref=ybuf.at[target],
            dst_ref=zbuf.at[step],
            send_sem=ysend.at[step],
            recv_sem=yrecv.at[step],
            device_id=(me, target),
            device_id_type=MESH,
        )

    for t in range(tiles):
        picked = xall[(me - pairs[1, t] + BLKS) % BLKS].astype(F32) * mask[0, t].astype(F32)
        ybuf[:, t] = picked.astype(BF16).reshape(GRPS, ROWS, T)
    for step in range(1, GRPS):
        slice_copy(step).start()
    for step in range(1, GRPS):
        slice_copy(step).wait_recv()
    total = ybuf[grp].astype(F32)
    for step in range(1, GRPS):
        total = total + zbuf[step].astype(F32)
    acc[0:tiles] = total
    acc[tiles] = jnp.zeros((ROWS, T), F32)

    def owned_copy(step):
        target = (me + step) % BLKS
        return pltpu.make_async_remote_copy(
            src_ref=obuf.at[target],
            dst_ref=out.at[0, me],
            send_sem=osend.at[step],
            recv_sem=orecv.at[step],
            device_id=(target, grp),
            device_id_type=MESH,
        )

    def owned_arrival(step):
        source = (me + BLKS - step) % BLKS
        return pltpu.make_async_remote_copy(
            src_ref=obuf.at[source],
            dst_ref=out.at[0, source],
            send_sem=osend.at[step],
            recv_sem=orecv.at[step],
            device_id=(source, grp),
            device_id_type=MESH,
        )

    for o in range(BLKS):
        for c in range(SLOTS):
            obuf[o, c] = acc[tbl[o * 2 + c]]
    for step in range(1, BLKS):
        owned_copy(step).start()
    keep = pltpu.make_async_copy(obuf.at[me], out.at[0, me], osem)
    keep.start()

    for k in range(1, CHIPS):
        raw_copy(k).wait_send()
        partial_copy(k).wait_send()
    for k in range(CHIPS):
        fitted_copy(k).wait_send()
    for j in range(1, HALF):
        cross_copy(j).wait_send()
    for step in range(1, GRPS):
        slice_copy(step).wait_send()
    keep.wait()
    for step in range(1, BLKS):
        owned_arrival(step).wait_recv()
        owned_copy(step).wait_send()


def per_device(raw_panels, metric, tile_pairs, owners, group_mask):
    tiles = tile_pairs.shape[0]
    dma = pltpu.SemaphoreType.DMA
    any_space = pl.BlockSpec(memory_space=pl.ANY)
    smem = pl.BlockSpec(memory_space=pltpu.SMEM)
    return pl.pallas_call(
        kernel,
        out_shape=jax.ShapeDtypeStruct((1, BLKS, SLOTS, ROWS, T), F32),
        in_specs=[any_space, any_space, smem, smem, smem],
        out_specs=any_space,
        scratch_shapes=[
            pltpu.VMEM((K, K), BF16),
            pltpu.VMEM((CHIPS, T, K), BF16),
            pltpu.VMEM((BLKS, T, K), BF16),
            pltpu.VMEM((CHIPS, HALF, T, T), BF16),
            pltpu.VMEM((CHIPS, HALF, T, T), BF16),
            pltpu.VMEM((HALF, T, T), BF16),
            pltpu.VMEM((BLKS, T, T), BF16),
            pltpu.VMEM((GRPS, tiles, ROWS, T), BF16),
            pltpu.VMEM((GRPS, tiles, ROWS, T), BF16),
            pltpu.VMEM((tiles + 1, ROWS, T), F32),
            pltpu.VMEM((BLKS, SLOTS, ROWS, T), F32),
            pltpu.SMEM((BLKS * SLOTS,), jnp.int32),
            dma(()), dma(()),
            dma((CHIPS,)), dma((CHIPS,)),
            dma((CHIPS,)), dma((CHIPS,)),
            dma((CHIPS,)), dma((CHIPS,)),
            dma((HALF,)), dma((HALF,)),
            dma((GRPS,)), dma((GRPS,)),
            dma((BLKS,)), dma((BLKS,)),
            dma(()),
        ],
        compiler_params=pltpu.CompilerParams(collective_id=0, has_side_effects=True, vmem_limit_bytes=60 << 20),
        name="exchange",
    )(raw_panels[0], metric, tile_pairs.T, owners.T, group_mask.T)


def solution(mesh):
    placed = (P("grp", "blk", None), P(), P("blk", None), P("blk", None), P("blk", "grp"))
    return jax.shard_map(
        per_device,
        mesh=mesh,
        in_specs=placed,
        out_specs=P("blk", None, None, "grp", None),
        check_vma=False,
    )
```

```python
import jax
import jax.numpy as jnp
from jax import lax
from jax.experimental import pallas as pl
from jax.experimental.pallas import tpu as pltpu
from jax.sharding import PartitionSpec as P

MESH = pl.DeviceIdType.MESH
F32, BF16 = jnp.float32, jnp.bfloat16

CHIPS = 8
BLKS = 16
GRPS = 8
T = 128
K = 1024
HALF = 8
SLOTS = 2
ROWS = T // GRPS
PARTS = 4
PART = T // PARTS
NEAR = (2, 6, 1, 5, 3, 7, 4)
ORDER = (2, 4, 6, 1, 3, 5, 7, 8)
STARTS = (0, 2, 4, 7, 8)
QS = len(STARTS) - 1
LIMIT = 60


def dot_t(a, b):
    return lax.dot_general(a, b, (((1,), (1,)), ((), ())), preferred_element_type=F32)


def kernel(
    raw, metric, pairs, owners, mask, out,
    met, rbuf, fbuf, sbuf, pbuf, xs, xall, zbuf, acc, obuf, mvec, msc, tbl, place,
    msem, lsem, vsem, asend, arecv, fsend, frecv, psend, precv, xsend, xrecv, ysend, yrecv, osend, orecv, ksend, krecv, osem,
):
    me = lax.axis_index("blk")
    grp = lax.axis_index("grp")
    chip, core = me // 2, me % 2
    cx, cy = chip // 2, chip % 2
    tiles = pairs.shape[1]

    def chip_to(k):
        return ((cx + k // 2) % 4) * 2 + (cy + k % 2) % 2

    def chip_from(k):
        return ((cx + 4 - k // 2) % 4) * 2 + (cy + k % 2) % 2

    fetch_metric = pltpu.make_async_copy(metric, met, msem)
    fetch_metric.start()
    own = pltpu.make_async_copy(raw.at[:, pl.ds(pl.multiple_of(chip * K, K), K)], rbuf.at[0], lsem)
    own.start()
    own_mask = pltpu.make_async_copy(mask, mvec.at[0], vsem)
    own_mask.start()

    barrier = pltpu.get_barrier_semaphore()
    for step in range(1, BLKS):
        pl.semaphore_signal(barrier, inc=1, device_id=((me + step) % BLKS, grp), device_id_type=MESH)
    for step in range(1, GRPS):
        pl.semaphore_signal(barrier, inc=1, device_id=(me, (grp + step) % GRPS), device_id_type=MESH)
    pl.semaphore_wait(barrier, BLKS - 1 + GRPS - 1)

    def raw_copy(part, k):
        target = chip_to(k)
        rows = pl.ds(pl.multiple_of(part * PART, PART), PART)
        return pltpu.make_async_remote_copy(
            src_ref=raw.at[rows, pl.ds(pl.multiple_of(target * K, K), K)],
            dst_ref=rbuf.at[k, rows],
            send_sem=asend.at[part, k],
            recv_sem=arecv.at[part, k],
            device_id=(target * 2 + core, grp),
            device_id_type=MESH,
        )

    for part in range(PARTS):
        for k in NEAR:
            raw_copy(part, k).start()

    def mask_copy(step):
        return pltpu.make_async_remote_copy(
            src_ref=mask,
            dst_ref=mvec.at[step],
            send_sem=ksend.at[step],
            recv_sem=krecv.at[step],
            device_id=(me, (grp + step) % GRPS),
            device_id_type=MESH,
        )

    for step in range(1, GRPS):
        mask_copy(step).start()

    def find(o, carry):
        seen, first, second = jnp.int32(0), jnp.int32(tiles), jnp.int32(tiles)
        for t in range(tiles):
            hit = (owners[0, t] == o).astype(jnp.int32)
            first = first + hit * (seen == 0).astype(jnp.int32) * (t - tiles)
            second = second + hit * (seen == 1).astype(jnp.int32) * (t - tiles)
            seen = seen + hit
        tbl[o * 2] = first
        tbl[o * 2 + 1] = second
        return carry

    lax.fori_loop(0, BLKS, find, 0)
    place[0] = 0
    for u, j in enumerate(ORDER):
        place[j] = u
        if j < HALF:
            place[BLKS - j] = HALF + u

    def fitted_copy(part, parity):
        rows = fbuf.at[:, parity, pl.ds(pl.multiple_of(part * PART, PART), PART)]
        return pltpu.make_async_remote_copy(
            src_ref=rows,
            dst_ref=rows,
            send_sem=fsend.at[part],
            recv_sem=frecv.at[part],
            device_id=(chip * 2 + 1 - core, grp),
            device_id_type=MESH,
        )

    fetch_metric.wait()
    own.wait()

    def fit(part, carry):
        for k in NEAR:
            raw_copy(part, k).wait_recv()
        rows = pl.ds(pl.multiple_of(part * PART, PART), PART)
        fitted = dot_t(rbuf[:, rows, :].reshape(CHIPS * PART, K), met[...]).astype(BF16).reshape(CHIPS, PART, K)
        for k in range(CHIPS):
            fbuf[chip_from(k), core, rows, :] = fitted[k]
        fitted_copy(part, core).start()
        return carry

    lax.fori_loop(0, PARTS, fit, 0)

    def partial_copy(q, k):
        which = pl.ds(STARTS[q], STARTS[q + 1] - STARTS[q])
        return pltpu.make_async_remote_copy(
            src_ref=sbuf.at[k, which],
            dst_ref=pbuf.at[k, which],
            send_sem=psend.at[q, k],
            recv_sem=precv.at[q, k],
            device_id=(chip_to(k) * 2 + core, grp),
            device_id_type=MESH,
        )

    def products(q):
        def multiply(step, carry):
            k = (step + 1) % CHIPS
            target = chip_to(k)
            reducer = target * 2 + core
            right = fbuf[target, core]
            for u in range(STARTS[q], STARTS[q + 1]):
                block = (reducer + ORDER[u]) % BLKS
                sbuf[k, u] = dot_t(fbuf[block // 2, block % 2], right).astype(BF16)

            @pl.when(k > 0)
            def _():
                partial_copy(q, k).start()

            return carry

        lax.fori_loop(0, CHIPS, multiply, 0)

    def cross_copy(u):
        return pltpu.make_async_remote_copy(
            src_ref=xs.at[u],
            dst_ref=xall.at[HALF + u],
            send_sem=xsend.at[u],
            recv_sem=xrecv.at[u],
            device_id=((me + ORDER[u]) % BLKS, grp),
            device_id_type=MESH,
        )

    def slice_copy(n, first, last, step):
        target = (grp + step) % GRPS
        which = pl.ds(first, last - first)
        return pltpu.make_async_remote_copy(
            src_ref=xall.at[which, pl.ds(pl.multiple_of(target * ROWS, ROWS), ROWS)],
            dst_ref=zbuf.at[step, which],
            send_sem=ysend.at[n, step],
            recv_sem=yrecv.at[n, step],
            device_id=(me, target),
            device_id_type=MESH,
        )

    slices = []

    def send_slices(first, last):
        n = len(slices)
        slices.append((n, first, last))
        for step in range(1, GRPS):
            slice_copy(n, first, last, step).start()

    def reduce(q):
        for k in NEAR:
            partial_copy(q, k).wait_recv()
        for u in range(STARTS[q], STARTS[q + 1]):
            total = sbuf[0, u].astype(F32)
            for k in range(1, CHIPS):
                total = total + pbuf[k, u].astype(F32)
            if ORDER[u] < HALF:
                xs[u] = total.astype(BF16)
                cross_copy(u).start()
            xall[u] = total.T.astype(BF16)
        send_slices(STARTS[q], STARTS[q + 1])

    def crossed(q):
        for u in range(STARTS[q], STARTS[q + 1]):
            cross_copy(u).wait_recv()
        send_slices(HALF + STARTS[q], HALF + STARTS[q + 1])

    products(0)
    for part in range(PARTS):
        fitted_copy(part, 1 - core).wait_recv()
    for q in range(1, QS):
        products(q)
    for q in range(QS):
        reduce(q)
        if q > 0:
            crossed(q - 1)

    for step in range(1, GRPS):
        mask_copy(step).wait_recv()
    own_mask.wait()
    masks = pltpu.make_async_copy(mvec, msc, vsem)
    masks.start()
    masks.wait()
    for n, first, last in slices:
        for step in range(1, GRPS):
            slice_copy(n, first, last, step).wait_recv()
    own_rows = pl.ds(pl.multiple_of(grp * ROWS, ROWS), ROWS)
    for t in range(tiles):
        at = place[(pairs[1, t] - me + BLKS) % BLKS]
        total = xall[at, own_rows, :].astype(F32) * msc[0, 0, t].astype(F32)
        for step in range(1, GRPS):
            total = total + zbuf[step, at].astype(F32) * msc[step, 0, t].astype(F32)
        acc[t] = total
    acc[tiles] = jnp.zeros((ROWS, T), F32)

    def owned_copy(step):
        target = (me + step) % BLKS
        return pltpu.make_async_remote_copy(
            src_ref=obuf.at[target],
            dst_ref=out.at[0, me],
            send_sem=osend.at[step],
            recv_sem=orecv.at[step],
            device_id=(target, grp),
            device_id_type=MESH,
        )

    def owned_arrival(step):
        source = (me + BLKS - step) % BLKS
        return pltpu.make_async_remote_copy(
            src_ref=obuf.at[source],
            dst_ref=out.at[0, source],
            send_sem=osend.at[step],
            recv_sem=orecv.at[step],
            device_id=(source, grp),
            device_id_type=MESH,
        )

    for step in range(BLKS):
        o = (me + step) % BLKS
        for c in range(SLOTS):
            obuf[o, c] = acc[tbl[o * 2 + c]]
        if step > 0:
            owned_copy(step).start()
    keep = pltpu.make_async_copy(obuf.at[me], out.at[0, me], osem)
    keep.start()

    for part in range(PARTS):
        for k in NEAR:
            raw_copy(part, k).wait_send()
        fitted_copy(part, core).wait_send()
    for q in range(QS):
        for k in NEAR:
            partial_copy(q, k).wait_send()
    for u in range(HALF):
        if ORDER[u] < HALF:
            cross_copy(u).wait_send()
    for step in range(1, GRPS):
        mask_copy(step).wait_send()
        for n, first, last in slices:
            slice_copy(n, first, last, step).wait_send()
    keep.wait()
    for step in range(1, BLKS):
        owned_arrival(step).wait_recv()
        owned_copy(step).wait_send()


def per_device(raw_panels, metric, tile_pairs, owners, group_mask):
    tiles = tile_pairs.shape[0]
    dma = pltpu.SemaphoreType.DMA
    any_space = pl.BlockSpec(memory_space=pl.ANY)
    hbm = pl.BlockSpec(memory_space=pltpu.HBM)
    smem = pl.BlockSpec(memory_space=pltpu.SMEM)
    return pl.pallas_call(
        kernel,
        out_shape=jax.ShapeDtypeStruct((1, BLKS, SLOTS, ROWS, T), F32),
        in_specs=[hbm, hbm, smem, smem, hbm],
        out_specs=any_space,
        scratch_shapes=[
            pltpu.VMEM((K, K), BF16),
            pltpu.VMEM((CHIPS, T, K), BF16),
            pltpu.VMEM((CHIPS, 2, T, K), BF16),
            pltpu.VMEM((CHIPS, HALF, T, T), BF16),
            pltpu.VMEM((CHIPS, HALF, T, T), BF16),
            pltpu.VMEM((HALF, T, T), BF16),
            pltpu.VMEM((BLKS, T, T), BF16),
            pltpu.VMEM((GRPS, BLKS, ROWS, T), BF16),
            pltpu.VMEM((tiles + 1, ROWS, T), F32),
            pltpu.VMEM((BLKS, SLOTS, ROWS, T), F32),
            pltpu.VMEM((GRPS, 1, tiles), jnp.int32),
            pltpu.SMEM((GRPS, 1, tiles), jnp.int32),
            pltpu.SMEM((BLKS * SLOTS,), jnp.int32),
            pltpu.SMEM((BLKS,), jnp.int32),
            dma(()), dma(()), dma(()),
            dma((PARTS, CHIPS)), dma((PARTS, CHIPS)),
            dma((PARTS,)), dma((PARTS,)),
            dma((QS, CHIPS)), dma((QS, CHIPS)),
            dma((HALF,)), dma((HALF,)),
            dma((2 * QS - 1, GRPS)), dma((2 * QS - 1, GRPS)),
            dma((BLKS,)), dma((BLKS,)),
            dma((GRPS,)), dma((GRPS,)),
            dma(()),
        ],
        compiler_params=pltpu.CompilerParams(collective_id=0, has_side_effects=True, vmem_limit_bytes=LIMIT << 20),
        name="exchange",
    )(raw_panels[0], metric, tile_pairs.T, owners.T, group_mask.T)


def solution(mesh):
    placed = (P("grp", "blk", None), P(), P("blk", None), P("blk", None), P("blk", "grp"))
    return jax.shard_map(
        per_device,
        mesh=mesh,
        in_specs=placed,
        out_specs=P("blk", None, None, "grp", None),
        check_vma=False,
    )
```

```python
import jax
import jax.numpy as jnp
from jax import lax
from jax.experimental import pallas as pl
from jax.experimental.pallas import tpu as pltpu
from jax.sharding import PartitionSpec as P

MESH = pl.DeviceIdType.MESH
F32, BF16 = jnp.float32, jnp.bfloat16

CHIPS = 8
BLKS = 16
GRPS = 8
T = 128
K = 1024
HALF = 8
SLOTS = 2
ROWS = T // GRPS
PARTS = 4
PART = T // PARTS
NEAR = (2, 6, 1, 5, 3, 7, 4)
ORDER = (2, 4, 6, 1, 3, 5, 7, 8)
STARTS = (0, 2, 4, 7, 8)
QS = len(STARTS) - 1
AHEAD = 3
LIMIT = 60


def dot_t(a, b):
    return lax.dot_general(a, b, (((1,), (1,)), ((), ())), preferred_element_type=F32)


def kernel(
    raw, metric, pairs, owners, mask, out,
    met, rbuf, fbuf, sbuf, pbuf, xs, xall, zbuf, acc, obuf, mvec, msc, tbl, place,
    msem, lsem, vsem, asend, arecv, fsend, frecv, psend, precv, xsend, xrecv, ysend, yrecv, osend, orecv, ksend, krecv, osem,
):
    me = lax.axis_index("blk")
    grp = lax.axis_index("grp")
    chip, core = me // 2, me % 2
    cx, cy = chip // 2, chip % 2
    tiles = pairs.shape[1]

    def chip_to(k):
        return ((cx + k // 2) % 4) * 2 + (cy + k % 2) % 2

    def chip_from(k):
        return ((cx + 4 - k // 2) % 4) * 2 + (cy + k % 2) % 2

    fetch_metric = pltpu.make_async_copy(metric, met, msem)
    fetch_metric.start()
    own = pltpu.make_async_copy(raw.at[:, pl.ds(pl.multiple_of(chip * K, K), K)], rbuf.at[0], lsem)
    own.start()
    own_mask = pltpu.make_async_copy(mask, mvec.at[0], vsem)
    own_mask.start()

    barrier = pltpu.get_barrier_semaphore()
    for step in range(1, BLKS):
        pl.semaphore_signal(barrier, inc=1, device_id=((me + step) % BLKS, grp), device_id_type=MESH)
    for step in range(1, GRPS):
        pl.semaphore_signal(barrier, inc=1, device_id=(me, (grp + step) % GRPS), device_id_type=MESH)
    pl.semaphore_wait(barrier, BLKS - 1 + GRPS - 1)

    def raw_copy(part, k):
        target = chip_to(k)
        rows = pl.ds(pl.multiple_of(part * PART, PART), PART)
        return pltpu.make_async_remote_copy(
            src_ref=raw.at[rows, pl.ds(pl.multiple_of(target * K, K), K)],
            dst_ref=rbuf.at[k, rows],
            send_sem=asend.at[part, k],
            recv_sem=arecv.at[part, k],
            device_id=(target * 2 + core, grp),
            device_id_type=MESH,
        )

    for part in range(PARTS):
        for k in NEAR:
            raw_copy(part, k).start()

    def mask_copy(step):
        return pltpu.make_async_remote_copy(
            src_ref=mask,
            dst_ref=mvec.at[step],
            send_sem=ksend.at[step],
            recv_sem=krecv.at[step],
            device_id=(me, (grp + step) % GRPS),
            device_id_type=MESH,
        )

    for step in range(1, GRPS):
        mask_copy(step).start()

    def find(o, carry):
        seen, first, second = jnp.int32(0), jnp.int32(tiles), jnp.int32(tiles)
        for t in range(tiles):
            hit = (owners[0, t] == o).astype(jnp.int32)
            first = first + hit * (seen == 0).astype(jnp.int32) * (t - tiles)
            second = second + hit * (seen == 1).astype(jnp.int32) * (t - tiles)
            seen = seen + hit
        tbl[o * 2] = first
        tbl[o * 2 + 1] = second
        return carry

    lax.fori_loop(0, BLKS, find, 0)
    place[0] = 0
    for u, j in enumerate(ORDER):
        place[j] = u
        if j < HALF:
            place[BLKS - j] = HALF + u

    def fitted_copy(part, parity):
        rows = fbuf.at[:, parity, pl.ds(pl.multiple_of(part * PART, PART), PART)]
        return pltpu.make_async_remote_copy(
            src_ref=rows,
            dst_ref=rows,
            send_sem=fsend.at[part],
            recv_sem=frecv.at[part],
            device_id=(chip * 2 + 1 - core, grp),
            device_id_type=MESH,
        )

    fetch_metric.wait()
    own.wait()

    def fit(part, carry):
        for k in NEAR:
            raw_copy(part, k).wait_recv()
        rows = pl.ds(pl.multiple_of(part * PART, PART), PART)
        fitted = dot_t(rbuf[:, rows, :].reshape(CHIPS * PART, K), met[...]).astype(BF16).reshape(CHIPS, PART, K)
        for k in range(CHIPS):
            fbuf[chip_from(k), core, rows, :] = fitted[k]
        fitted_copy(part, core).start()
        return carry

    lax.fori_loop(0, PARTS, fit, 0)

    def partial_copy(q, k):
        which = pl.ds(STARTS[q], STARTS[q + 1] - STARTS[q])
        return pltpu.make_async_remote_copy(
            src_ref=sbuf.at[k, which],
            dst_ref=pbuf.at[k, which],
            send_sem=psend.at[q, k],
            recv_sem=precv.at[q, k],
            device_id=(chip_to(k) * 2 + core, grp),
            device_id_type=MESH,
        )

    def products(q, send):
        def multiply(step, carry):
            k = (step + 1) % CHIPS
            target = chip_to(k)
            reducer = target * 2 + core
            right = fbuf[target, core]
            for u in range(STARTS[q], STARTS[q + 1]):
                block = (reducer + ORDER[u]) % BLKS
                sbuf[k, u] = dot_t(fbuf[block // 2, block % 2], right).astype(BF16)

            if send:

                @pl.when(k > 0)
                def _():
                    partial_copy(q, k).start()

            return carry

        lax.fori_loop(0, CHIPS, multiply, 0)

    def ship(q):
        for k in NEAR:
            partial_copy(q, k).start()

    def cross_copy(u, step):
        target = (grp + step) % GRPS
        return pltpu.make_async_remote_copy(
            src_ref=xs.at[u, pl.ds(pl.multiple_of(target * ROWS, ROWS), ROWS)],
            dst_ref=zbuf.at[step, HALF + u],
            send_sem=xsend.at[u, step],
            recv_sem=xrecv.at[u, step],
            device_id=((me + ORDER[u]) % BLKS, target),
            device_id_type=MESH,
        )

    def slice_copy(n, first, last, step):
        target = (grp + step) % GRPS
        which = pl.ds(first, last - first)
        return pltpu.make_async_remote_copy(
            src_ref=xall.at[which, pl.ds(pl.multiple_of(target * ROWS, ROWS), ROWS)],
            dst_ref=zbuf.at[step, which],
            send_sem=ysend.at[n, step],
            recv_sem=yrecv.at[n, step],
            device_id=(me, target),
            device_id_type=MESH,
        )

    slices = []

    def send_slices(first, last):
        n = len(slices)
        slices.append((n, first, last))
        for step in range(1, GRPS):
            slice_copy(n, first, last, step).start()

    own_rows = pl.ds(pl.multiple_of(grp * ROWS, ROWS), ROWS)

    def reduce(q):
        for k in NEAR:
            partial_copy(q, k).wait_recv()
        for u in range(STARTS[q], STARTS[q + 1]):
            total = sbuf[0, u].astype(F32)
            for k in range(1, CHIPS):
                total = total + pbuf[k, u].astype(F32)
            if ORDER[u] < HALF:
                xs[u] = total.astype(BF16)
                for step in range(GRPS):
                    cross_copy(u, step).start()
            xall[u] = total.T.astype(BF16)
            zbuf[0, u] = xall[u, own_rows, :]

    products(0, True)
    for part in range(PARTS):
        fitted_copy(part, 1 - core).wait_recv()
    for q in range(1, QS):
        products(q, q < AHEAD)
    for part in range(PARTS):
        for k in NEAR:
            raw_copy(part, k).wait_send()
        fitted_copy(part, core).wait_send()
    for step in range(1, GRPS):
        mask_copy(step).wait_send()
        mask_copy(step).wait_recv()
    own_mask.wait()
    masks = pltpu.make_async_copy(mvec, msc, vsem)
    masks.start()
    masks.wait()
    acc[tiles] = jnp.zeros((ROWS, T), F32)
    for q in range(QS):
        reduce(q)
        send_slices(STARTS[q], STARTS[q + 1])
        if q + AHEAD < QS:
            ship(q + AHEAD)

    for q in range(QS):
        for k in NEAR:
            partial_copy(q, k).wait_send()
    for n, first, last in slices:
        for step in range(1, GRPS):
            slice_copy(n, first, last, step).wait_recv()
    for u in range(HALF):
        if ORDER[u] < HALF:
            for step in range(GRPS):
                cross_copy(u, step).wait_recv()
    for t in range(tiles):
        at = place[(pairs[1, t] - me + BLKS) % BLKS]
        total = zbuf[0, at].astype(F32) * msc[0, 0, t].astype(F32)
        for step in range(1, GRPS):
            total = total + zbuf[step, at].astype(F32) * msc[step, 0, t].astype(F32)
        acc[t] = total

    def owned_copy(step):
        target = (me + step) % BLKS
        return pltpu.make_async_remote_copy(
            src_ref=obuf.at[target],
            dst_ref=out.at[0, me],
            send_sem=osend.at[step],
            recv_sem=orecv.at[step],
            device_id=(target, grp),
            device_id_type=MESH,
        )

    def owned_arrival(step):
        source = (me + BLKS - step) % BLKS
        return pltpu.make_async_remote_copy(
            src_ref=obuf.at[source],
            dst_ref=out.at[0, source],
            send_sem=osend.at[step],
            recv_sem=orecv.at[step],
            device_id=(source, grp),
            device_id_type=MESH,
        )

    for step in range(BLKS):
        o = (me + step) % BLKS
        for c in range(SLOTS):
            obuf[o, c] = acc[tbl[o * 2 + c]]
        if step > 0:
            owned_copy(step).start()
    keep = pltpu.make_async_copy(obuf.at[me], out.at[0, me], osem)
    keep.start()

    for u in range(HALF):
        if ORDER[u] < HALF:
            for step in range(GRPS):
                cross_copy(u, step).wait_send()
    for step in range(1, GRPS):
        for n, first, last in slices:
            slice_copy(n, first, last, step).wait_send()
    keep.wait()
    for step in range(1, BLKS):
        owned_arrival(step).wait_recv()
        owned_copy(step).wait_send()


def per_device(raw_panels, metric, tile_pairs, owners, group_mask):
    tiles = tile_pairs.shape[0]
    dma = pltpu.SemaphoreType.DMA
    any_space = pl.BlockSpec(memory_space=pl.ANY)
    hbm = pl.BlockSpec(memory_space=pltpu.HBM)
    smem = pl.BlockSpec(memory_space=pltpu.SMEM)
    return pl.pallas_call(
        kernel,
        out_shape=jax.ShapeDtypeStruct((1, BLKS, SLOTS, ROWS, T), F32),
        in_specs=[hbm, hbm, smem, smem, hbm],
        out_specs=any_space,
        scratch_shapes=[
            pltpu.VMEM((K, K), BF16),
            pltpu.VMEM((CHIPS, T, K), BF16),
            pltpu.VMEM((CHIPS, 2, T, K), BF16),
            pltpu.VMEM((CHIPS, HALF, T, T), BF16),
            pltpu.VMEM((CHIPS, HALF, T, T), BF16),
            pltpu.VMEM((HALF, T, T), BF16),
            pltpu.VMEM((HALF, T, T), BF16),
            pltpu.VMEM((GRPS, BLKS, ROWS, T), BF16),
            pltpu.VMEM((tiles + 1, ROWS, T), F32),
            pltpu.VMEM((BLKS, SLOTS, ROWS, T), F32),
            pltpu.VMEM((GRPS, 1, tiles), jnp.int32),
            pltpu.SMEM((GRPS, 1, tiles), jnp.int32),
            pltpu.SMEM((BLKS * SLOTS,), jnp.int32),
            pltpu.SMEM((BLKS,), jnp.int32),
            dma(()), dma(()), dma(()),
            dma((PARTS, CHIPS)), dma((PARTS, CHIPS)),
            dma((PARTS,)), dma((PARTS,)),
            dma((QS, CHIPS)), dma((QS, CHIPS)),
            dma((HALF, GRPS)), dma((HALF, GRPS)),
            dma((QS, GRPS)), dma((QS, GRPS)),
            dma((BLKS,)), dma((BLKS,)),
            dma((GRPS,)), dma((GRPS,)),
            dma(()),
        ],
        compiler_params=pltpu.CompilerParams(collective_id=0, has_side_effects=True, vmem_limit_bytes=LIMIT << 20),
        name="exchange",
    )(raw_panels[0], metric, tile_pairs.T, owners.T, group_mask.T)


def solution(mesh):
    placed = (P("grp", "blk", None), P(), P("blk", None), P("blk", None), P("blk", "grp"))
    return jax.shard_map(
        per_device,
        mesh=mesh,
        in_specs=placed,
        out_specs=P("blk", None, None, "grp", None),
        check_vma=False,
    )
```

```python
import jax
import jax.numpy as jnp
from jax import lax
from jax.experimental import pallas as pl
from jax.experimental.pallas import tpu as pltpu
from jax.sharding import PartitionSpec as P

MESH = pl.DeviceIdType.MESH
F32, BF16 = jnp.float32, jnp.bfloat16

CHIPS = 8
BLKS = 16
GRPS = 8
T = 128
K = 1024
HALF = 8
SLOTS = 2
ROWS = T // GRPS
PARTS = 4
PART = T // PARTS
NEAR = (2, 6, 1, 5, 3, 7, 4)
ORDER = (2, 4, 6, 1, 3, 5, 7, 8)
STARTS = (0, 3, 6, 7, 8)
QS = len(STARTS) - 1
REACHED = (CHIPS, CHIPS, CHIPS, CHIPS // 2)
LIMIT = 60


def dot_t(a, b):
    return lax.dot_general(a, b, (((1,), (1,)), ((), ())), preferred_element_type=F32)


def kernel(
    raw, metric, pairs, owners, mask, out,
    met, rbuf, fbuf, sbuf, pbuf, xs, xall, zbuf, acc, obuf, mvec, msc, tbl, place,
    msem, lsem, vsem, asend, arecv, fsend, frecv, psend, precv, xsend, xrecv, ysend, yrecv, osend, orecv, ksend, krecv, osem,
):
    me = lax.axis_index("blk")
    grp = lax.axis_index("grp")
    chip, core = me // 2, me % 2
    cx, cy = chip // 2, chip % 2
    tiles = pairs.shape[1]

    def chip_to(k):
        return ((cx + k // 2) % 4) * 2 + (cy + k % 2) % 2

    def chip_from(k):
        return ((cx + 4 - k // 2) % 4) * 2 + (cy + k % 2) % 2

    barrier = pltpu.get_barrier_semaphore()
    for step in range(1, BLKS):
        pl.semaphore_signal(barrier, inc=1, device_id=((me + step) % BLKS, grp), device_id_type=MESH)
    for step in range(1, GRPS):
        pl.semaphore_signal(barrier, inc=1, device_id=(me, (grp + step) % GRPS), device_id_type=MESH)
    fetch_metric = pltpu.make_async_copy(metric, met, msem)
    fetch_metric.start()
    own = pltpu.make_async_copy(raw.at[:, pl.ds(pl.multiple_of(chip * K, K), K)], rbuf.at[0], lsem)
    own.start()
    own_mask = pltpu.make_async_copy(mask, mvec.at[0], vsem)
    own_mask.start()
    pl.semaphore_wait(barrier, BLKS - 1 + GRPS - 1)

    def raw_copy(part, k):
        target = chip_to(k)
        rows = pl.ds(pl.multiple_of(part * PART, PART), PART)
        return pltpu.make_async_remote_copy(
            src_ref=raw.at[rows, pl.ds(pl.multiple_of(target * K, K), K)],
            dst_ref=rbuf.at[k, rows],
            send_sem=asend.at[part, k],
            recv_sem=arecv.at[part, k],
            device_id=(target * 2 + core, grp),
            device_id_type=MESH,
        )

    for part in range(PARTS):
        for k in NEAR:
            raw_copy(part, k).start()

    def mask_copy(step):
        return pltpu.make_async_remote_copy(
            src_ref=mask,
            dst_ref=mvec.at[step],
            send_sem=ksend.at[step],
            recv_sem=krecv.at[step],
            device_id=(me, (grp + step) % GRPS),
            device_id_type=MESH,
        )

    for step in range(1, GRPS):
        mask_copy(step).start()

    def find(o, carry):
        seen, first, second = jnp.int32(0), jnp.int32(tiles), jnp.int32(tiles)
        for t in range(tiles):
            hit = (owners[0, t] == o).astype(jnp.int32)
            first = first + hit * (seen == 0).astype(jnp.int32) * (t - tiles)
            second = second + hit * (seen == 1).astype(jnp.int32) * (t - tiles)
            seen = seen + hit
        tbl[o * 2] = first
        tbl[o * 2 + 1] = second
        return carry

    lax.fori_loop(0, BLKS, find, 0)
    place[0] = 0
    for u, j in enumerate(ORDER):
        place[j] = u
        if j < HALF:
            place[BLKS - j] = HALF + u

    def fitted_copy(part, parity):
        rows = fbuf.at[:, parity, pl.ds(pl.multiple_of(part * PART, PART), PART)]
        return pltpu.make_async_remote_copy(
            src_ref=rows,
            dst_ref=rows,
            send_sem=fsend.at[part],
            recv_sem=frecv.at[part],
            device_id=(chip * 2 + 1 - core, grp),
            device_id_type=MESH,
        )

    fetch_metric.wait()
    own.wait()

    def fit(part, carry):
        for k in NEAR:
            raw_copy(part, k).wait_recv()
        rows = pl.ds(pl.multiple_of(part * PART, PART), PART)
        fitted = dot_t(rbuf[:, rows, :].reshape(CHIPS * PART, K), met[...]).astype(BF16).reshape(CHIPS, PART, K)
        for k in range(CHIPS):
            fbuf[chip_from(k), core, rows, :] = fitted[k]
        fitted_copy(part, core).start()
        return carry

    lax.fori_loop(0, PARTS, fit, 0)

    def reach(q, n):
        return n if q < QS - 1 else n + n // 2 * 4 * core

    def partial_copy(q, n):
        which = pl.ds(STARTS[q], STARTS[q + 1] - STARTS[q])
        return pltpu.make_async_remote_copy(
            src_ref=sbuf.at[n, which],
            dst_ref=pbuf.at[n, which],
            send_sem=psend.at[q, n],
            recv_sem=precv.at[q, n],
            device_id=(chip_to(reach(q, n)) * 2 + core, grp),
            device_id_type=MESH,
        )

    def products(q):
        def multiply(step, carry):
            n = (step + 1) % REACHED[q]
            target = chip_to(reach(q, n))
            reducer = target * 2 + core
            right = fbuf[target, core]
            for u in range(STARTS[q], STARTS[q + 1]):
                block = (reducer + ORDER[u]) % BLKS
                sbuf[n, u] = dot_t(fbuf[block // 2, block % 2], right).astype(BF16)

            @pl.when(n > 0)
            def _():
                partial_copy(q, n).start()

            return carry

        lax.fori_loop(0, REACHED[q], multiply, 0)

    def cross_copy(u, step):
        target = (grp + step) % GRPS
        return pltpu.make_async_remote_copy(
            src_ref=xs.at[u, pl.ds(pl.multiple_of(target * ROWS, ROWS), ROWS)],
            dst_ref=zbuf.at[step, HALF + u],
            send_sem=xsend.at[u, step],
            recv_sem=xrecv.at[u, step],
            device_id=((me + ORDER[u]) % BLKS, target),
            device_id_type=MESH,
        )

    def slice_copy(n, first, last, step):
        target = (grp + step) % GRPS
        which = pl.ds(first, last - first)
        return pltpu.make_async_remote_copy(
            src_ref=xall.at[which, pl.ds(pl.multiple_of(target * ROWS, ROWS), ROWS)],
            dst_ref=zbuf.at[step, which],
            send_sem=ysend.at[n, step],
            recv_sem=yrecv.at[n, step],
            device_id=(me, target),
            device_id_type=MESH,
        )

    slices = []

    def send_slices(first, last):
        n = len(slices)
        slices.append((n, first, last))
        for step in range(1, GRPS):
            slice_copy(n, first, last, step).start()

    own_rows = pl.ds(pl.multiple_of(grp * ROWS, ROWS), ROWS)

    def reduce(q):
        for n in range(1, REACHED[q]):
            partial_copy(q, n).wait_recv()
        for u in range(STARTS[q], STARTS[q + 1]):
            total = sbuf[0, u].astype(F32)
            for n in range(1, REACHED[q]):
                total = total + pbuf[n, u].astype(F32)
            xs[u] = total.astype(BF16)
            for step in range(GRPS):
                cross_copy(u, step).start()
            xall[u] = total.T.astype(BF16)
            zbuf[0, u] = xall[u, own_rows, :]

    products(0)
    for part in range(PARTS):
        fitted_copy(part, 1 - core).wait_recv()
    for q in range(1, QS):
        products(q)
    for part in range(PARTS):
        for k in NEAR:
            raw_copy(part, k).wait_send()
        fitted_copy(part, core).wait_send()
    for step in range(1, GRPS):
        mask_copy(step).wait_send()
        mask_copy(step).wait_recv()
    own_mask.wait()
    masks = pltpu.make_async_copy(mvec, msc, vsem)
    masks.start()
    masks.wait()
    acc[tiles] = jnp.zeros((ROWS, T), F32)
    for q in range(QS):
        reduce(q)
        if q == QS - 3:
            send_slices(0, STARTS[q + 1])
        if q == QS - 1:
            send_slices(STARTS[q - 1], HALF)

    for q in range(QS):
        for n in range(1, REACHED[q]):
            partial_copy(q, n).wait_send()
    for n, first, last in slices:
        for step in range(1, GRPS):
            slice_copy(n, first, last, step).wait_recv()
    for u in range(HALF):
        for step in range(GRPS):
            cross_copy(u, step).wait_recv()
    for t in range(tiles):
        apart = (pairs[1, t] - me + BLKS) % BLKS
        at = place[apart]
        both = (apart == HALF).astype(F32)
        total = jnp.zeros((ROWS, T), F32)
        for step in range(GRPS):
            value = zbuf[step, at].astype(F32) + zbuf[step, BLKS - 1].astype(F32) * both
            total = total + value * msc[step, 0, t].astype(F32)
        acc[t] = total

    def owned_copy(step):
        target = (me + step) % BLKS
        return pltpu.make_async_remote_copy(
            src_ref=obuf.at[target],
            dst_ref=out.at[0, me],
            send_sem=osend.at[step],
            recv_sem=orecv.at[step],
            device_id=(target, grp),
            device_id_type=MESH,
        )

    def owned_arrival(step):
        source = (me + BLKS - step) % BLKS
        return pltpu.make_async_remote_copy(
            src_ref=obuf.at[source],
            dst_ref=out.at[0, source],
            send_sem=osend.at[step],
            recv_sem=orecv.at[step],
            device_id=(source, grp),
            device_id_type=MESH,
        )

    for step in range(BLKS):
        o = (me + step) % BLKS
        for c in range(SLOTS):
            obuf[o, c] = acc[tbl[o * 2 + c]]
        if step > 0:
            owned_copy(step).start()
    keep = pltpu.make_async_copy(obuf.at[me], out.at[0, me], osem)
    keep.start()

    for u in range(HALF):
        for step in range(GRPS):
            cross_copy(u, step).wait_send()
    for step in range(1, GRPS):
        for n, first, last in slices:
            slice_copy(n, first, last, step).wait_send()
    keep.wait()
    for step in range(1, BLKS):
        owned_arrival(step).wait_recv()
        owned_copy(step).wait_send()


def per_device(raw_panels, metric, tile_pairs, owners, group_mask):
    tiles = tile_pairs.shape[0]
    dma = pltpu.SemaphoreType.DMA
    any_space = pl.BlockSpec(memory_space=pl.ANY)
    hbm = pl.BlockSpec(memory_space=pltpu.HBM)
    smem = pl.BlockSpec(memory_space=pltpu.SMEM)
    return pl.pallas_call(
        kernel,
        out_shape=jax.ShapeDtypeStruct((1, BLKS, SLOTS, ROWS, T), F32),
        in_specs=[hbm, hbm, smem, smem, hbm],
        out_specs=any_space,
        scratch_shapes=[
            pltpu.VMEM((K, K), BF16),
            pltpu.VMEM((CHIPS, T, K), BF16),
            pltpu.VMEM((CHIPS, 2, T, K), BF16),
            pltpu.VMEM((CHIPS, HALF, T, T), BF16),
            pltpu.VMEM((CHIPS, HALF, T, T), BF16),
            pltpu.VMEM((HALF, T, T), BF16),
            pltpu.VMEM((HALF, T, T), BF16),
            pltpu.VMEM((GRPS, BLKS, ROWS, T), BF16),
            pltpu.VMEM((tiles + 1, ROWS, T), F32),
            pltpu.VMEM((BLKS, SLOTS, ROWS, T), F32),
            pltpu.VMEM((GRPS, 1, tiles), jnp.int32),
            pltpu.SMEM((GRPS, 1, tiles), jnp.int32),
            pltpu.SMEM((BLKS * SLOTS,), jnp.int32),
            pltpu.SMEM((BLKS,), jnp.int32),
            dma(()), dma(()), dma(()),
            dma((PARTS, CHIPS)), dma((PARTS, CHIPS)),
            dma((PARTS,)), dma((PARTS,)),
            dma((QS, CHIPS)), dma((QS, CHIPS)),
            dma((HALF, GRPS)), dma((HALF, GRPS)),
            dma((QS, GRPS)), dma((QS, GRPS)),
            dma((BLKS,)), dma((BLKS,)),
            dma((GRPS,)), dma((GRPS,)),
            dma(()),
        ],
        compiler_params=pltpu.CompilerParams(collective_id=0, has_side_effects=True, vmem_limit_bytes=LIMIT << 20),
        name="exchange",
    )(raw_panels[0], metric, tile_pairs.T, owners.T, group_mask.T)


def solution(mesh):
    placed = (P("grp", "blk", None), P(), P("blk", None), P("blk", None), P("blk", "grp"))
    return jax.shard_map(
        per_device,
        mesh=mesh,
        in_specs=placed,
        out_specs=P("blk", None, None, "grp", None),
        check_vma=False,
    )
```

```python
import jax
import jax.numpy as jnp
from jax import lax
from jax.experimental import pallas as pl
from jax.experimental.pallas import tpu as pltpu
from jax.sharding import PartitionSpec as P

MESH = pl.DeviceIdType.MESH
F32, BF16 = jnp.float32, jnp.bfloat16

CHIPS = 8
BLKS = 16
GRPS = 8
T = 128
K = 1024
HALF = 8
SLOTS = 2
ROWS = T // GRPS
PARTS = 4
PART = T // PARTS
NEAR = (2, 6, 1, 5, 3, 7, 4)
ORDER = (2, 4, 6, 1, 3, 5, 7, 8)
STARTS = (0, 3, 6, 7, 8)
QS = len(STARTS) - 1
REACHED = (CHIPS, CHIPS, CHIPS, CHIPS // 2)
LIMIT = 60


def dot_t(a, b):
    return lax.dot_general(a, b, (((1,), (1,)), ((), ())), preferred_element_type=F32)


def kernel(
    raw, metric, pairs, owners, mask, out,
    met, rbuf, fbuf, sbuf, pbuf, xs, xall, zbuf, acc, obuf, mvec, msc, tbl, place,
    msem, lsem, vsem, asend, arecv, fsend, frecv, psend, precv, xsend, xrecv, ysend, yrecv, osend, orecv, ksend, krecv, osem,
):
    me = lax.axis_index("blk")
    grp = lax.axis_index("grp")
    chip, core = me // 2, me % 2
    cx, cy = chip // 2, chip % 2
    tiles = pairs.shape[1]

    def chip_to(k):
        return ((cx + k // 2) % 4) * 2 + (cy + k % 2) % 2

    def chip_from(k):
        return ((cx + 4 - k // 2) % 4) * 2 + (cy + k % 2) % 2

    barrier = pltpu.get_barrier_semaphore()
    for step in range(1, BLKS):
        pl.semaphore_signal(barrier, inc=1, device_id=((me + step) % BLKS, grp), device_id_type=MESH)
    for step in range(1, GRPS):
        pl.semaphore_signal(barrier, inc=1, device_id=(me, (grp + step) % GRPS), device_id_type=MESH)
    fetch_metric = pltpu.make_async_copy(metric, met, msem)
    fetch_metric.start()
    own = pltpu.make_async_copy(raw.at[:, pl.ds(pl.multiple_of(chip * K, K), K)], rbuf.at[0], lsem)
    own.start()
    own_mask = pltpu.make_async_copy(mask, mvec.at[0], vsem)
    own_mask.start()
    pl.semaphore_wait(barrier, BLKS - 1 + GRPS - 1)

    def raw_copy(part, k):
        target = chip_to(k)
        rows = pl.ds(pl.multiple_of(part * PART, PART), PART)
        return pltpu.make_async_remote_copy(
            src_ref=raw.at[rows, pl.ds(pl.multiple_of(target * K, K), K)],
            dst_ref=rbuf.at[k, rows],
            send_sem=asend.at[part, k],
            recv_sem=arecv.at[part, k],
            device_id=(target * 2 + core, grp),
            device_id_type=MESH,
        )

    for part in range(PARTS):
        for k in NEAR:
            raw_copy(part, k).start()

    def mask_copy(step):
        return pltpu.make_async_remote_copy(
            src_ref=mask,
            dst_ref=mvec.at[step],
            send_sem=ksend.at[step],
            recv_sem=krecv.at[step],
            device_id=(me, (grp + step) % GRPS),
            device_id_type=MESH,
        )

    for step in range(1, GRPS):
        mask_copy(step).start()

    def find(o, carry):
        seen, first, second = jnp.int32(0), jnp.int32(tiles), jnp.int32(tiles)
        for t in range(tiles):
            hit = (owners[0, t] == o).astype(jnp.int32)
            first = first + hit * (seen == 0).astype(jnp.int32) * (t - tiles)
            second = second + hit * (seen == 1).astype(jnp.int32) * (t - tiles)
            seen = seen + hit
        tbl[o * 2] = first
        tbl[o * 2 + 1] = second
        return carry

    lax.fori_loop(0, BLKS, find, 0)
    place[0] = 0
    for u, j in enumerate(ORDER):
        place[j] = u
        if j < HALF:
            place[BLKS - j] = HALF + u

    def fitted_copy(part, parity):
        rows = fbuf.at[:, parity, pl.ds(pl.multiple_of(part * PART, PART), PART)]
        return pltpu.make_async_remote_copy(
            src_ref=rows,
            dst_ref=rows,
            send_sem=fsend.at[part],
            recv_sem=frecv.at[part],
            device_id=(chip * 2 + 1 - core, grp),
            device_id_type=MESH,
        )

    fetch_metric.wait()
    own.wait()

    def fit(part, carry):
        for k in NEAR:
            raw_copy(part, k).wait_recv()
        rows = pl.ds(pl.multiple_of(part * PART, PART), PART)
        fitted = dot_t(rbuf[:, rows, :].reshape(CHIPS * PART, K), met[...]).astype(BF16).reshape(CHIPS, PART, K)
        for k in range(CHIPS):
            fbuf[chip_from(k), core, rows, :] = fitted[k]
        fitted_copy(part, core).start()
        return carry

    lax.fori_loop(0, PARTS, fit, 0)

    def reach(q, n):
        return n if q < QS - 1 else n + n // 2 * 4 * core

    def partial_copy(q, n):
        which = pl.ds(STARTS[q], STARTS[q + 1] - STARTS[q])
        return pltpu.make_async_remote_copy(
            src_ref=sbuf.at[n, which],
            dst_ref=pbuf.at[n, which],
            send_sem=psend.at[q, n],
            recv_sem=precv.at[q, n],
            device_id=(chip_to(reach(q, n)) * 2 + core, grp),
            device_id_type=MESH,
        )

    def products(q):
        def multiply(step, carry):
            n = (step + 1) % REACHED[q]
            target = chip_to(reach(q, n))
            reducer = target * 2 + core
            right = fbuf[target, core]
            for u in range(STARTS[q], STARTS[q + 1]):
                block = (reducer + ORDER[u]) % BLKS
                sbuf[n, u] = dot_t(fbuf[block // 2, block % 2], right).astype(BF16)

            @pl.when(n > 0)
            def _():
                partial_copy(q, n).start()

            return carry

        lax.fori_loop(0, REACHED[q], multiply, 0)

    def cross_copy(u, step):
        target = (grp + step) % GRPS
        return pltpu.make_async_remote_copy(
            src_ref=xs.at[u, pl.ds(pl.multiple_of(target * ROWS, ROWS), ROWS)],
            dst_ref=zbuf.at[step, HALF + u],
            send_sem=xsend.at[u, step],
            recv_sem=xrecv.at[u, step],
            device_id=((me + ORDER[u]) % BLKS, target),
            device_id_type=MESH,
        )

    def slice_copy(n, first, last, step):
        target = (grp + step) % GRPS
        which = pl.ds(first, last - first)
        return pltpu.make_async_remote_copy(
            src_ref=xall.at[which, pl.ds(pl.multiple_of(target * ROWS, ROWS), ROWS)],
            dst_ref=zbuf.at[step, which],
            send_sem=ysend.at[n, step],
            recv_sem=yrecv.at[n, step],
            device_id=(me, target),
            device_id_type=MESH,
        )

    slices = []

    def send_slices(first, last):
        n = len(slices)
        slices.append((n, first, last))
        for step in range(1, GRPS):
            slice_copy(n, first, last, step).start()

    own_rows = pl.ds(pl.multiple_of(grp * ROWS, ROWS), ROWS)

    def reduce(q):
        for n in range(1, REACHED[q]):
            partial_copy(q, n).wait_recv()
        for u in range(STARTS[q], STARTS[q + 1]):
            total = sbuf[0, u].astype(F32)
            for n in range(1, REACHED[q]):
                total = total + pbuf[n, u].astype(F32)
            xs[u] = total.astype(BF16)
            for step in (4, 5, 3, 2, 6, 7, 1, 0):
                cross_copy(u, step).start()
            xall[u] = total.T.astype(BF16)

    products(0)
    for part in range(PARTS):
        fitted_copy(part, 1 - core).wait_recv()
    for q in range(1, QS):
        products(q)
    for part in range(PARTS):
        for k in NEAR:
            raw_copy(part, k).wait_send()
        fitted_copy(part, core).wait_send()
    for step in range(1, GRPS):
        mask_copy(step).wait_send()
        mask_copy(step).wait_recv()
    own_mask.wait()
    masks = pltpu.make_async_copy(mvec, msc, vsem)
    masks.start()
    masks.wait()
    acc[tiles] = jnp.zeros((ROWS, T), F32)
    for q in range(QS):
        reduce(q)
        if q == QS - 3:
            send_slices(0, STARTS[q + 1])
        if q == QS - 1:
            send_slices(STARTS[q - 1], HALF)
            for u in range(HALF):
                zbuf[0, u] = xall[u, own_rows, :]

    for q in range(QS):
        for n in range(1, REACHED[q]):
            partial_copy(q, n).wait_send()
    for n, first, last in slices:
        for step in range(1, GRPS):
            slice_copy(n, first, last, step).wait_recv()
    for u in range(HALF):
        for step in range(GRPS):
            cross_copy(u, step).wait_recv()
    for t in range(tiles):
        apart = (pairs[1, t] - me + BLKS) % BLKS
        at = place[apart]
        both = (apart == HALF).astype(F32)
        total = jnp.zeros((ROWS, T), F32)
        for step in range(GRPS):
            value = zbuf[step, at].astype(F32) + zbuf[step, BLKS - 1].astype(F32) * both
            total = total + value * msc[step, 0, t].astype(F32)
        acc[t] = total

    def owned_copy(step):
        target = (me + step) % BLKS
        return pltpu.make_async_remote_copy(
            src_ref=obuf.at[target],
            dst_ref=out.at[0, me],
            send_sem=osend.at[step],
            recv_sem=orecv.at[step],
            device_id=(target, grp),
            device_id_type=MESH,
        )

    def owned_arrival(step):
        source = (me + BLKS - step) % BLKS
        return pltpu.make_async_remote_copy(
            src_ref=obuf.at[source],
            dst_ref=out.at[0, source],
            send_sem=osend.at[step],
            recv_sem=orecv.at[step],
            device_id=(source, grp),
            device_id_type=MESH,
        )

    for step in (8, 10, 6, 9, 7, 11, 5, 12, 4, 3, 13, 2, 14, 15, 1, 0):
        o = (me + step) % BLKS
        for c in range(SLOTS):
            obuf[o, c] = acc[tbl[o * 2 + c]]
        if step > 0:
            owned_copy(step).start()
    keep = pltpu.make_async_copy(obuf.at[me], out.at[0, me], osem)
    keep.start()

    for u in range(HALF):
        for step in range(GRPS):
            cross_copy(u, step).wait_send()
    for step in range(1, GRPS):
        for n, first, last in slices:
            slice_copy(n, first, last, step).wait_send()
    keep.wait()
    for step in range(1, BLKS):
        owned_arrival(step).wait_recv()
        owned_copy(step).wait_send()


def per_device(raw_panels, metric, tile_pairs, owners, group_mask):
    tiles = tile_pairs.shape[0]
    dma = pltpu.SemaphoreType.DMA
    any_space = pl.BlockSpec(memory_space=pl.ANY)
    hbm = pl.BlockSpec(memory_space=pltpu.HBM)
    smem = pl.BlockSpec(memory_space=pltpu.SMEM)
    return pl.pallas_call(
        kernel,
        out_shape=jax.ShapeDtypeStruct((1, BLKS, SLOTS, ROWS, T), F32),
        in_specs=[hbm, hbm, smem, smem, hbm],
        out_specs=any_space,
        scratch_shapes=[
            pltpu.VMEM((K, K), BF16),
            pltpu.VMEM((CHIPS, T, K), BF16),
            pltpu.VMEM((CHIPS, 2, T, K), BF16),
            pltpu.VMEM((CHIPS, HALF, T, T), BF16),
            pltpu.VMEM((CHIPS, HALF, T, T), BF16),
            pltpu.VMEM((HALF, T, T), BF16),
            pltpu.VMEM((HALF, T, T), BF16),
            pltpu.VMEM((GRPS, BLKS, ROWS, T), BF16),
            pltpu.VMEM((tiles + 1, ROWS, T), F32),
            pltpu.VMEM((BLKS, SLOTS, ROWS, T), F32),
            pltpu.VMEM((GRPS, 1, tiles), jnp.int32),
            pltpu.SMEM((GRPS, 1, tiles), jnp.int32),
            pltpu.SMEM((BLKS * SLOTS,), jnp.int32),
            pltpu.SMEM((BLKS,), jnp.int32),
            dma(()), dma(()), dma(()),
            dma((PARTS, CHIPS)), dma((PARTS, CHIPS)),
            dma((PARTS,)), dma((PARTS,)),
            dma((QS, CHIPS)), dma((QS, CHIPS)),
            dma((HALF, GRPS)), dma((HALF, GRPS)),
            dma((QS, GRPS)), dma((QS, GRPS)),
            dma((BLKS,)), dma((BLKS,)),
            dma((GRPS,)), dma((GRPS,)),
            dma(()),
        ],
        compiler_params=pltpu.CompilerParams(collective_id=0, has_side_effects=True, vmem_limit_bytes=LIMIT << 20),
        name="exchange",
    )(raw_panels[0], metric, tile_pairs.T, owners.T, group_mask.T)


def solution(mesh):
    placed = (P("grp", "blk", None), P(), P("blk", None), P("blk", None), P("blk", "grp"))
    return jax.shard_map(
        per_device,
        mesh=mesh,
        in_specs=placed,
        out_specs=P("blk", None, None, "grp", None),
        check_vma=False,
    )
```

```python
import jax
import jax.numpy as jnp
from jax import lax
from jax.experimental import pallas as pl
from jax.experimental.pallas import tpu as pltpu
from jax.sharding import PartitionSpec as P

MESH = pl.DeviceIdType.MESH
F32, BF16 = jnp.float32, jnp.bfloat16

CHIPS = 8
BLKS = 16
GRPS = 8
T = 128
K = 1024
HALF = 8
SLOTS = 2
ROWS = T // GRPS
PARTS = 4
PART = T // PARTS
NEAR = (2, 6, 1, 5, 3, 7, 4)
ORDER = (2, 4, 6, 1, 3, 5, 7, 8)
STARTS = (0, 2, 6, 7, 8)
QS = len(STARTS) - 1
REACHED = (CHIPS, CHIPS, CHIPS, CHIPS // 2)
LIMIT = 60


def dot_t(a, b):
    return lax.dot_general(a, b, (((1,), (1,)), ((), ())), preferred_element_type=F32)


def kernel(
    raw, metric, pairs, owners, mask, out,
    met, rbuf, fbuf, sbuf, pbuf, xs, xall, zbuf, acc, obuf, mvec, msc, tbl, place,
    msem, lsem, vsem, asend, arecv, fsend, frecv, psend, precv, xsend, xrecv, ysend, yrecv, osend, orecv, ksend, krecv, osem,
):
    me = lax.axis_index("blk")
    grp = lax.axis_index("grp")
    chip, core = me // 2, me % 2
    cx, cy = chip // 2, chip % 2
    tiles = pairs.shape[1]

    def chip_to(k):
        return ((cx + k // 2) % 4) * 2 + (cy + k % 2) % 2

    def chip_from(k):
        return ((cx + 4 - k // 2) % 4) * 2 + (cy + k % 2) % 2

    barrier = pltpu.get_barrier_semaphore()
    for step in range(1, BLKS):
        pl.semaphore_signal(barrier, inc=1, device_id=((me + step) % BLKS, grp), device_id_type=MESH)
    for step in range(1, GRPS):
        pl.semaphore_signal(barrier, inc=1, device_id=(me, (grp + step) % GRPS), device_id_type=MESH)
    fetch_metric = pltpu.make_async_copy(metric, met, msem)
    fetch_metric.start()
    own = pltpu.make_async_copy(raw.at[:, pl.ds(pl.multiple_of(chip * K, K), K)], rbuf.at[0], lsem)
    own.start()
    own_mask = pltpu.make_async_copy(mask, mvec.at[0], vsem)
    own_mask.start()
    pl.semaphore_wait(barrier, BLKS - 1 + GRPS - 1)

    def raw_copy(part, k):
        target = chip_to(k)
        rows = pl.ds(pl.multiple_of(part * PART, PART), PART)
        return pltpu.make_async_remote_copy(
            src_ref=raw.at[rows, pl.ds(pl.multiple_of(target * K, K), K)],
            dst_ref=rbuf.at[k, rows],
            send_sem=asend.at[part, k],
            recv_sem=arecv.at[part, k],
            device_id=(target * 2 + core, grp),
            device_id_type=MESH,
        )

    for part in range(PARTS):
        for k in NEAR:
            raw_copy(part, k).start()

    def mask_copy(step):
        return pltpu.make_async_remote_copy(
            src_ref=mask,
            dst_ref=mvec.at[step],
            send_sem=ksend.at[step],
            recv_sem=krecv.at[step],
            device_id=(me, (grp + step) % GRPS),
            device_id_type=MESH,
        )

    for step in range(1, GRPS):
        mask_copy(step).start()

    def find(o, carry):
        seen, first, second = jnp.int32(0), jnp.int32(tiles), jnp.int32(tiles)
        for t in range(tiles):
            hit = (owners[0, t] == o).astype(jnp.int32)
            first = first + hit * (seen == 0).astype(jnp.int32) * (t - tiles)
            second = second + hit * (seen == 1).astype(jnp.int32) * (t - tiles)
            seen = seen + hit
        tbl[o * 2] = first
        tbl[o * 2 + 1] = second
        return carry

    lax.fori_loop(0, BLKS, find, 0)
    place[0] = 0
    for u, j in enumerate(ORDER):
        place[j] = u
        if j < HALF:
            place[BLKS - j] = HALF + u

    def fitted_copy(part, parity):
        rows = fbuf.at[:, parity, pl.ds(pl.multiple_of(part * PART, PART), PART)]
        return pltpu.make_async_remote_copy(
            src_ref=rows,
            dst_ref=rows,
            send_sem=fsend.at[part],
            recv_sem=frecv.at[part],
            device_id=(chip * 2 + 1 - core, grp),
            device_id_type=MESH,
        )

    fetch_metric.wait()
    own.wait()

    def fit(part, carry):
        for k in NEAR:
            raw_copy(part, k).wait_recv()
        rows = pl.ds(pl.multiple_of(part * PART, PART), PART)
        fitted = dot_t(rbuf[:, rows, :].reshape(CHIPS * PART, K), met[...]).astype(BF16).reshape(CHIPS, PART, K)
        for k in range(CHIPS):
            fbuf[chip_from(k), core, rows, :] = fitted[k]
        fitted_copy(part, core).start()
        return carry

    lax.fori_loop(0, PARTS, fit, 0)

    def reach(q, n):
        return n if q < QS - 1 else n + n // 2 * 4 * core

    def partial_copy(q, n):
        which = pl.ds(STARTS[q], STARTS[q + 1] - STARTS[q])
        return pltpu.make_async_remote_copy(
            src_ref=sbuf.at[n, which],
            dst_ref=pbuf.at[n, which],
            send_sem=psend.at[q, n],
            recv_sem=precv.at[q, n],
            device_id=(chip_to(reach(q, n)) * 2 + core, grp),
            device_id_type=MESH,
        )

    def products(q):
        def multiply(step, carry):
            n = (step + 1) % REACHED[q]
            target = chip_to(reach(q, n))
            reducer = target * 2 + core
            right = fbuf[target, core]
            for u in range(STARTS[q], STARTS[q + 1]):
                block = (reducer + ORDER[u]) % BLKS
                sbuf[n, u] = dot_t(fbuf[block // 2, block % 2], right).astype(BF16)

            @pl.when(n > 0)
            def _():
                partial_copy(q, n).start()

            return carry

        lax.fori_loop(0, REACHED[q], multiply, 0)

    def cross_copy(u, step):
        target = (grp + step) % GRPS
        return pltpu.make_async_remote_copy(
            src_ref=xs.at[u, pl.ds(pl.multiple_of(target * ROWS, ROWS), ROWS)],
            dst_ref=zbuf.at[step, HALF + u],
            send_sem=xsend.at[u, step],
            recv_sem=xrecv.at[u, step],
            device_id=((me + ORDER[u]) % BLKS, target),
            device_id_type=MESH,
        )

    def slice_copy(n, first, last, step):
        target = (grp + step) % GRPS
        which = pl.ds(first, last - first)
        return pltpu.make_async_remote_copy(
            src_ref=xall.at[which, pl.ds(pl.multiple_of(target * ROWS, ROWS), ROWS)],
            dst_ref=zbuf.at[step, which],
            send_sem=ysend.at[n, step],
            recv_sem=yrecv.at[n, step],
            device_id=(me, target),
            device_id_type=MESH,
        )

    slices = []

    def send_slices(first, last):
        n = len(slices)
        slices.append((n, first, last))
        for step in range(1, GRPS):
            slice_copy(n, first, last, step).start()

    own_rows = pl.ds(pl.multiple_of(grp * ROWS, ROWS), ROWS)

    def reduce(q):
        for n in range(1, REACHED[q]):
            partial_copy(q, n).wait_recv()
        for u in range(STARTS[q], STARTS[q + 1]):
            total = sbuf[0, u].astype(F32)
            for n in range(1, REACHED[q]):
                total = total + pbuf[n, u].astype(F32)
            xs[u] = total.astype(BF16)
            for step in (4, 5, 3, 2, 6, 7, 1, 0):
                cross_copy(u, step).start()
            xall[u] = total.T.astype(BF16)

    products(0)
    for part in range(PARTS):
        fitted_copy(part, 1 - core).wait_recv()
    for q in range(1, QS):
        products(q)
    for part in range(PARTS):
        for k in NEAR:
            raw_copy(part, k).wait_send()
        fitted_copy(part, core).wait_send()
    for step in range(1, GRPS):
        mask_copy(step).wait_send()
        mask_copy(step).wait_recv()
    own_mask.wait()
    masks = pltpu.make_async_copy(mvec, msc, vsem)
    masks.start()
    masks.wait()
    acc[tiles] = jnp.zeros((ROWS, T), F32)
    for q in range(QS):
        reduce(q)
        if q == QS - 3:
            send_slices(0, STARTS[q + 1])
        if q == QS - 1:
            send_slices(STARTS[q - 1], HALF)
            for u in range(HALF):
                zbuf[0, u] = xall[u, own_rows, :]

    for q in range(QS):
        for n in range(1, REACHED[q]):
            partial_copy(q, n).wait_send()
    for n, first, last in slices:
        for step in range(1, GRPS):
            slice_copy(n, first, last, step).wait_recv()
    for u in range(HALF):
        for step in range(GRPS):
            cross_copy(u, step).wait_recv()
    for t in range(tiles):
        apart = (pairs[1, t] - me + BLKS) % BLKS
        at = place[apart]
        both = (apart == HALF).astype(F32)
        total = jnp.zeros((ROWS, T), F32)
        for step in range(GRPS):
            value = zbuf[step, at].astype(F32) + zbuf[step, BLKS - 1].astype(F32) * both
            total = total + value * msc[step, 0, t].astype(F32)
        acc[t] = total

    def owned_copy(step):
        target = (me + step) % BLKS
        return pltpu.make_async_remote_copy(
            src_ref=obuf.at[target],
            dst_ref=out.at[0, me],
            send_sem=osend.at[step],
            recv_sem=orecv.at[step],
            device_id=(target, grp),
            device_id_type=MESH,
        )

    def owned_arrival(step):
        source = (me + BLKS - step) % BLKS
        return pltpu.make_async_remote_copy(
            src_ref=obuf.at[source],
            dst_ref=out.at[0, source],
            send_sem=osend.at[step],
            recv_sem=orecv.at[step],
            device_id=(source, grp),
            device_id_type=MESH,
        )

    for step in (8, 10, 6, 9, 7, 11, 5, 12, 4, 3, 13, 2, 14, 15, 1, 0):
        o = (me + step) % BLKS
        for c in range(SLOTS):
            obuf[o, c] = acc[tbl[o * 2 + c]]
        if step > 0:
            owned_copy(step).start()
    keep = pltpu.make_async_copy(obuf.at[me], out.at[0, me], osem)
    keep.start()

    for u in range(HALF):
        for step in range(GRPS):
            cross_copy(u, step).wait_send()
    for step in range(1, GRPS):
        for n, first, last in slices:
            slice_copy(n, first, last, step).wait_send()
    keep.wait()
    for step in range(1, BLKS):
        owned_arrival(step).wait_recv()
        owned_copy(step).wait_send()


def per_device(raw_panels, metric, tile_pairs, owners, group_mask):
    tiles = tile_pairs.shape[0]
    dma = pltpu.SemaphoreType.DMA
    any_space = pl.BlockSpec(memory_space=pl.ANY)
    hbm = pl.BlockSpec(memory_space=pltpu.HBM)
    smem = pl.BlockSpec(memory_space=pltpu.SMEM)
    return pl.pallas_call(
        kernel,
        out_shape=jax.ShapeDtypeStruct((1, BLKS, SLOTS, ROWS, T), F32),
        in_specs=[hbm, hbm, smem, smem, hbm],
        out_specs=any_space,
        scratch_shapes=[
            pltpu.VMEM((K, K), BF16),
            pltpu.VMEM((CHIPS, T, K), BF16),
            pltpu.VMEM((CHIPS, 2, T, K), BF16),
            pltpu.VMEM((CHIPS, HALF, T, T), BF16),
            pltpu.VMEM((CHIPS, HALF, T, T), BF16),
            pltpu.VMEM((HALF, T, T), BF16),
            pltpu.VMEM((HALF, T, T), BF16),
            pltpu.VMEM((GRPS, BLKS, ROWS, T), BF16),
            pltpu.VMEM((tiles + 1, ROWS, T), F32),
            pltpu.VMEM((BLKS, SLOTS, ROWS, T), F32),
            pltpu.VMEM((GRPS, 1, tiles), jnp.int32),
            pltpu.SMEM((GRPS, 1, tiles), jnp.int32),
            pltpu.SMEM((BLKS * SLOTS,), jnp.int32),
            pltpu.SMEM((BLKS,), jnp.int32),
            dma(()), dma(()), dma(()),
            dma((PARTS, CHIPS)), dma((PARTS, CHIPS)),
            dma((PARTS,)), dma((PARTS,)),
            dma((QS, CHIPS)), dma((QS, CHIPS)),
            dma((HALF, GRPS)), dma((HALF, GRPS)),
            dma((QS, GRPS)), dma((QS, GRPS)),
            dma((BLKS,)), dma((BLKS,)),
            dma((GRPS,)), dma((GRPS,)),
            dma(()),
        ],
        compiler_params=pltpu.CompilerParams(collective_id=0, has_side_effects=True, vmem_limit_bytes=LIMIT << 20),
        name="exchange",
    )(raw_panels[0], metric, tile_pairs.T, owners.T, group_mask.T)


def solution(mesh):
    placed = (P("grp", "blk", None), P(), P("blk", None), P("blk", None), P("blk", "grp"))
    return jax.shard_map(
        per_device,
        mesh=mesh,
        in_specs=placed,
        out_specs=P("blk", None, None, "grp", None),
        check_vma=False,
    )
```
